512 devices in a mesh: branch: 8 (over z_lo), dp: 64 (over x, y, z_hi, core).
Axes of the slice: x: 4, y: 4, z: 16 (z_hi: 2, z_lo: 8; z = z_hi * 8 + z_lo), core: 2. Of those that a mesh axis runs over, the one named last changes fastest.
Arguments:
- tokens: bfloat16 [512, 4096], P('dp'), may hold values from -6 to 6
- routes: int32 [512, 2], P('dp'), may hold values from 0 to 7, all different within a row; in each aligned block of 8 rows (0 to 7, 8 to 15, ...) at most 4 rows name the same one
- route_weights: float32 [512, 2], P('dp'), may hold values from 0.2 to 1
- norm_gains: float32 [8, 4096], P('branch'), may hold values from 0.25 to 1.75
- keyval_weights: bfloat16 [8, 4096, 2048], P('branch', 'dp'), may hold values from -0.09375 to 0.09375
- expert_gate: bfloat16 [8, 4096, 8192], P('branch', None, 'dp'), may hold values from -0.09375 to 0.09375
- expert_up: bfloat16 [8, 4096, 8192], P('branch', None, 'dp'), may hold values from -0.09375 to 0.09375
- expert_down: bfloat16 [8, 8192, 4096], P('branch', None, 'dp'), may hold values from -0.0625 to 0.0625
Outputs:
- mixed: bfloat16 [512, 4096], P('dp')
- merged_keyval: bfloat16 [4096, 2048], P('dp', 'branch')
The draws below stay inside these ranges and needn't reach their ends.
Inputs may be any that keep to these rules, and one draw needn't show every extreme that they name: `routes`: each token names 2 different experts. Among the 8 tokens of one dp index at most 4 name one expert, a bound that some block reaches.
All inputs are finite; a program needn't handle non-finite values.
Results may differ from the reference program's by a relative error of at most 0.013.
Values may be sent and summed in bfloat16 or wider, within the bound.
No kernel may reach another device: no remote copies, remote signals or barrier semaphores. Data moves between devices by JAX's collectives and lax.ppermute only.
A program may use at most 64 MiB of HBM per device.

```python
import math
import jax
import jax.numpy as jnp
import numpy as np
from jax import lax

D = 4096
FFW = 8192
KVD = 1024
TOP = 2
TOK_DEV = 8
EXPERTS = 8
CAP = 4
TOKENS = 512
N_DP = 64


def block_scale(key, shape, cuts, low, top_value):
    level, own = 1.0, jax.random.fold_in(key, 6)
    for position, shards_of in cuts:
        heights = jnp.exp(jax.random.uniform(jax.random.fold_in(own, position), (shards_of,), jnp.float32, low / len(cuts), top_value / len(cuts)))
        level = level * jnp.repeat(heights, shape[position] // shards_of).reshape([-1 if axis == position else 1 for axis in range(len(shape))])
    return level


def assign_block(stream_key, own, number, rows, amount, top, most, skew):
    order = jax.random.permutation(stream_key, amount)
    crowded, usual = load_shares(amount, rows * top, most, skew, True), load_shares(amount, rows * top, most, skew, False)
    places = jnp.arange(amount)

    def named(tallies, offset_by):
        used = int((tallies > 0).sum())
        fixed = max(1, used // 4)
        shifted = fixed + (places - fixed + offset_by * (used - fixed)) % max(1, amount - fixed)
        return jnp.zeros((amount,), jnp.int32).at[order[jnp.where(places < fixed, places, shifted)]].set(jnp.asarray(tallies, jnp.int32))

    tallies = jnp.where(number % 4 == 0, named(crowded, number // 4), named(usual, number - number // 4 - 1))
    mixed = jax.random.permutation(jax.random.fold_in(own, 3), amount)
    donor, sink = mixed[0:amount // 2 * 2:2], mixed[1:amount // 2 * 2:2]
    slack = jnp.minimum(tallies[donor] - 1, most - tallies[sink]) // 2
    slack = jnp.where((donor == order[0]) | (sink == order[0]) | (tallies[sink] == 0), 0, jnp.maximum(slack, 0))
    shifted = jax.random.randint(jax.random.fold_in(own, 4), (amount // 2,), 0, 1 << 20) % (slack + 1)
    tallies = tallies.at[donor].add(-shifted).at[sink].add(shifted)
    labels = jnp.searchsorted(jnp.cumsum(tallies), jnp.arange(rows * top), side="right").astype(jnp.int32)
    table = labels.reshape(top, rows).T
    table = table[jax.random.permutation(jax.random.fold_in(own, 1), rows)]
    offset_by = jax.random.randint(jax.random.fold_in(own, 2), (rows, 1), 0, top)
    return jnp.take_along_axis(table, (jnp.arange(top)[None, :] + offset_by) % top, axis=1)


def load_shares(number_of, total, most, lean, full):
    loads = [(1 << 20) // math.isqrt(rank ** lean) + 1 for rank in range(1, number_of + 1)]
    largest = most if full else min(most, max(-(-total // number_of), total * loads[0] // sum(loads)))
    least = 1 if total - largest >= number_of - 1 else 0
    counts, surplus = [largest] + [least] * (number_of - 1), total - largest - least * (number_of - 1)
    while surplus > 0:
        movable = [i for i in range(1, number_of) if counts[i] < largest] or [i for i in range(1, number_of) if counts[i] < most]
        mass, remaining = sum([loads[i] for i in movable]), surplus
        for i in movable:
            more = min(most - counts[i], max(1, remaining * loads[i] // mass), surplus)
            counts[i] = counts[i] + more
            surplus = surplus - more
    return np.array(counts)


def bell_draw(key, extent, scale, bound, cuts=(), kind=jnp.bfloat16):
    loudness = block_scale(key, extent, cuts, -0.22, 0.18) if cuts else 1.0
    values = jax.random.normal(key, extent, jnp.float32) * scale * loudness
    return jnp.minimum(jnp.maximum(values, -bound), bound).astype(kind)


def setup_inputs(seed: int = 0) -> dict:
    seeds = jax.random.split(jax.random.key(seed), 9)
    tokens = bell_draw(seeds[0], (TOKENS, D), 1.0, 6.0, ((0, 64),))
    routes_keys = jax.random.split(jax.random.fold_in(seeds[1], 1), TOKENS // TOK_DEV)
    routes_turns = jax.random.permutation(jax.random.fold_in(seeds[1], 3), TOKENS // TOK_DEV)
    routes = jax.vmap(lambda own, number: assign_block(jax.random.fold_in(seeds[1], 2), own, number, TOK_DEV, EXPERTS, TOP, CAP, 2))(routes_keys, routes_turns).reshape((TOKENS, TOP))
    route_weights = jnp.clip(0.2 + 0.8 * jax.random.uniform(seeds[2], (TOKENS, TOP), jnp.float32) ** block_scale(seeds[2], (TOKENS, TOP), ((0, 64),), -0.2, 0.2), 0.2, 1.0)
    norm_gains = jnp.clip(1.0 + 0.15 * jax.random.normal(seeds[3], (EXPERTS, D), jnp.float32), 0.25, 1.75)
    keyval_weights = bell_draw(seeds[4], (EXPERTS, D, 2 * KVD), D ** -0.5, 0.09375, ((0, 8), (1, 64)))
    expert_gate = bell_draw(seeds[5], (EXPERTS, D, FFW), D ** -0.5, 0.09375, ((0, 8), (2, 64)))
    expert_up = bell_draw(seeds[6], (EXPERTS, D, FFW), D ** -0.5, 0.09375, ((0, 8), (2, 64)))
    expert_down = bell_draw(seeds[7], (EXPERTS, FFW, D), FFW ** -0.5, 0.0625, ((0, 8), (2, 64)))
    return dict(tokens=tokens, routes=routes, route_weights=route_weights, norm_gains=norm_gains, keyval_weights=keyval_weights, expert_gate=expert_gate, expert_up=expert_up, expert_down=expert_down)


def reference(tokens, routes, route_weights, norm_gains, keyval_weights, expert_gate, expert_up, expert_down):
    gain_avg = lax.optimization_barrier(jnp.mean(norm_gains, axis=0))
    merged_keyval = lax.optimization_barrier(jnp.mean(keyval_weights.astype(jnp.float32), axis=0)).astype(jnp.bfloat16)
    widened = tokens.astype(jnp.float32)
    inv_rms = lax.rsqrt(lax.optimization_barrier(jnp.mean(widened * widened, axis=1, keepdims=True)) + 1e-05)
    normed = (widened * inv_rms * gain_avg[None, :]).astype(jnp.bfloat16)
    capacity = min(TOK_DEV, 4 * TOK_DEV // EXPERTS)
    shard_rows = normed.astype(jnp.float32).reshape(N_DP, TOK_DEV, D)
    route_shards = routes.reshape(N_DP, TOK_DEV, TOP)
    weight_shards = route_weights.reshape(N_DP, TOK_DEV, TOP)
    running = jnp.zeros((N_DP, TOK_DEV, D), jnp.float32)
    for expert in range(EXPERTS):
        matched = route_shards == expert
        chosen = jnp.any(matched, axis=2)
        weight_share = lax.optimization_barrier(jnp.sum(jnp.where(matched, weight_shards, jnp.zeros_like(weight_shards)), axis=2))
        slot_index = jnp.cumsum(chosen.astype(jnp.int32), axis=1) - 1
        picks = ((slot_index[:, None, :] == jnp.arange(capacity, dtype=jnp.int32)[None, :, None]) & chosen[:, None, :]).astype(jnp.float32)
        packed = jnp.einsum('nct,ntd->ncd', picks, shard_rows).astype(jnp.bfloat16).reshape(N_DP * capacity, D)
        gate_part = jnp.dot(packed, expert_gate[expert], preferred_element_type=jnp.float32)
        up_part = jnp.dot(packed, expert_up[expert], preferred_element_type=jnp.float32)
        hidden = (jax.nn.silu(gate_part) * up_part).astype(jnp.bfloat16)
        result = jnp.dot(hidden, expert_down[expert], preferred_element_type=jnp.float32).astype(jnp.bfloat16)
        returned = jnp.einsum('nct,ncd->ntd', picks, result.astype(jnp.float32).reshape(N_DP, capacity, D))
        running = running + returned * weight_share[:, :, None]
    mixed = (widened + running.reshape(TOKENS, D)).astype(jnp.bfloat16)
    return (mixed, merged_keyval)
```

```python
import jax
import jax.numpy as jnp
from jax import lax
from jax.sharding import Mesh, PartitionSpec as P

F32 = jnp.float32
BF16 = jnp.bfloat16
XY = ("x", "y")
ZLINE = ("branch", "zh")
DP = ("x", "y", "zh", "core")
FLIP = [(0, 1), (1, 0)]


def route_tables(routes, route_weights, experts):
    matched = routes[:, :, None] == experts[None, None, :]
    chosen = jnp.any(matched, axis=1)
    share = jnp.sum(jnp.where(matched, route_weights[:, :, None], 0.0), axis=1)
    slot = jnp.cumsum(chosen.astype(jnp.int32), axis=0) - 1
    return chosen, share, slot


def local(
    tokens, routes, route_weights, norm_gains, keyval_weights, expert_gate, expert_up, expert_down
):
    experts = lax.axis_size("branch")
    n_xy = lax.axis_size("x") * lax.axis_size("y")
    expert = lax.axis_index("branch")
    half = lax.axis_index("zh")
    core = lax.axis_index("core")
    tok_count, width = tokens.shape
    cap = min(tok_count, 4 * tok_count // experts)
    group = 2 * cap

    wanted = jnp.stack([expert, (expert + experts // 2) % experts])
    chosen, _, slot = route_tables(routes, route_weights, wanted)
    rows = jnp.arange(group, dtype=jnp.int32)
    picks = (
        chosen.T[:, None, :]
        & (slot.T[:, None, :] == (rows % cap)[None, :, None])
        & (rows // cap == half)[None, :, None]
    ).astype(BF16)
    packed = jnp.dot(
        picks.reshape(2 * group, tok_count), tokens, preferred_element_type=F32
    ).astype(BF16)
    swap = [
        (2 * e + z, 2 * ((e + experts // 2) % experts) + 1 - z)
        for e in range(experts)
        for z in range(2)
    ]
    arrived = lax.ppermute(packed[group:], ZLINE, swap)
    both = packed[:group] + arrived
    spread = jnp.broadcast_to(both[None], (n_xy, group, width))
    mine = lax.all_to_all(spread, XY, 0, 0, tiled=True).reshape(n_xy * group, width)
    theirs = lax.ppermute(mine, "core", FLIP)

    kv = keyval_weights[0]
    kv_cols = kv.shape[1] // experts
    gain = norm_gains[0]
    gain_hi = lax.reduce_precision(gain, 8, 7)
    gain_lo = lax.reduce_precision(gain - gain_hi, 8, 7)
    gain_rows = jnp.stack([gain_hi, gain_lo]).astype(BF16).reshape(-1, kv_cols)
    kv_parts = kv.reshape(kv.shape[0], experts, kv_cols).swapaxes(0, 1)
    side = jnp.concatenate(
        [kv_parts, jnp.broadcast_to(gain_rows[None], (experts,) + gain_rows.shape)], axis=1
    )
    side = lax.all_to_all(side, "branch", 0, 0, tiled=True)
    side_sum = jnp.sum(side.astype(F32), axis=0) / experts
    merged_keyval = side_sum[: kv.shape[0]].astype(BF16)
    gain_avg = jnp.sum(side_sum[kv.shape[0] :].reshape(2, width), axis=0)

    def hidden_of(block):
        widened = block.astype(F32)
        inv_rms = lax.rsqrt(jnp.mean(widened * widened, axis=1, keepdims=True) + 1e-05)
        normed = (widened * inv_rms * gain_avg[None, :]).astype(BF16)
        gate = jnp.dot(normed, expert_gate[0], preferred_element_type=F32)
        up = jnp.dot(normed, expert_up[0], preferred_element_type=F32)
        return (jax.nn.silu(gate) * up).astype(BF16)

    hid_mine, hid_theirs = hidden_of(mine), hidden_of(theirs)
    units = hid_mine.shape[1]
    hid = jnp.stack(
        [
            jnp.where(core == 0, hid_mine, hid_theirs).reshape(n_xy, group, units),
            jnp.where(core == 0, hid_theirs, hid_mine).reshape(n_xy, group, units),
        ],
        axis=1,
    ).reshape(2 * n_xy * group, units)
    hid_far = lax.ppermute(hid, "zh", FLIP)
    hid = jnp.concatenate(
        [jnp.where(half == 0, hid, hid_far), jnp.where(half == 0, hid_far, hid)], axis=1
    )
    hid = lax.all_gather(hid, "core", axis=0, tiled=False)
    hid = jnp.concatenate([hid[0], hid[1]], axis=1)

    down = expert_down[0].T
    cols = down.shape[0]
    down = down.reshape(cols, n_xy, 2, 2, units).transpose(1, 0, 3, 2, 4)
    down = down.reshape(n_xy, cols, 4 * units)
    down = lax.all_to_all(down, XY, 0, 0, tiled=True).reshape(n_xy * cols, 4 * units)
    part = lax.dot_general(
        hid, down, (((1,), (1,)), ((), ())), preferred_element_type=F32
    ).astype(BF16)
    part = part.reshape(n_xy, 2 * group, n_xy * cols)
    part = lax.all_to_all(part, XY, 0, 0, tiled=True)
    total = jnp.sum(part.astype(F32), axis=0).astype(BF16)
    keep = jnp.where(core == 0, total[:group], total[group:])
    give = jnp.where(core == 0, total[group:], total[:group])
    got = lax.ppermute(give, "core", FLIP)
    whole = jnp.stack(
        [
            jnp.where(core == 0, keep, got).reshape(2, cap, n_xy, cols),
            jnp.where(core == 0, got, keep).reshape(2, cap, n_xy, cols),
        ],
        axis=3,
    ).reshape(2, cap, n_xy * 2 * cols)
    spread = jnp.broadcast_to(whole[None], (experts,) + whole.shape)
    spread = spread.reshape((2 * experts,) + whole.shape[1:])
    slots = lax.all_to_all(spread, ZLINE, 0, 0, tiled=True)
    slots = slots.reshape((experts, 2) + whole.shape[1:])

    chosen, share, slot = route_tables(routes, route_weights, jnp.arange(experts))
    mix = jnp.where(
        chosen[:, :, None] & (slot[:, :, None] == jnp.arange(cap)), share[:, :, None], 0.0
    )
    moe = jnp.einsum(
        "tes,ezsc->tzc", mix, slots.astype(F32), precision=lax.Precision.HIGHEST
    )
    moe = moe.reshape(tok_count, 2, n_xy, 2 * cols).swapaxes(1, 2).reshape(tok_count, width)
    mixed = (tokens.astype(F32) + moe).astype(BF16)
    return mixed, merged_keyval


def solution(mesh):
    n_x = n_y = int(round((mesh.devices.shape[1] // 4) ** 0.5))
    fine = Mesh(
        mesh.devices.reshape(mesh.devices.shape[0], n_x, n_y, 2, 2),
        ("branch", "x", "y", "zh", "core"),
    )
    in_specs = (
        P(DP, None),
        P(DP, None),
        P(DP, None),
        P("branch", None),
        P("branch", DP, None),
        P("branch", None, DP),
        P("branch", None, DP),
        P("branch", None, DP),
    )
    out_specs = (P(DP, None), P(DP, "branch"))
    return jax.shard_map(local, mesh=fine, in_specs=in_specs, out_specs=out_specs, check_vma=False)
```

```python
import functools

import jax
import jax.numpy as jnp
from jax import lax
from jax.experimental import pallas as pl
from jax.experimental.pallas import tpu as pltpu
from jax.sharding import Mesh, PartitionSpec as P

F32 = jnp.float32
BF16 = jnp.bfloat16
XY = ("x", "y")
ZLINE = ("branch", "zh")
DP = ("x", "y", "zh", "core")
FLIP = [(0, 1), (1, 0)]


def split_kernel(parts, source, target):
    span = source.shape[1] // parts
    for part in range(parts):
        target[part] = source[:, part * span : (part + 1) * span]


def split_columns(array, parts):
    rows, cols = array.shape
    return pl.pallas_call(
        functools.partial(split_kernel, parts),
        out_shape=jax.ShapeDtypeStruct((parts, rows, cols // parts), array.dtype),
        cost_estimate=pl.CostEstimate(
            flops=0, bytes_accessed=4 * rows * cols, transcendentals=0
        ),
        compiler_params=pltpu.CompilerParams(vmem_limit_bytes=8 << 20),
        name="split_columns",
    )(array)


def route_tables(routes, route_weights, experts):
    matched = routes[:, :, None] == experts[None, None, :]
    chosen = jnp.any(matched, axis=1)
    share = jnp.sum(jnp.where(matched, route_weights[:, :, None], 0.0), axis=1)
    slot = jnp.cumsum(chosen.astype(jnp.int32), axis=0) - 1
    return chosen, share, slot


def layer(
    tokens, routes, route_weights, norm_gains, keyval_weights, expert_gate, expert_up, expert_down
):
    experts = lax.axis_size("branch")
    n_xy = lax.axis_size("x") * lax.axis_size("y")
    expert = lax.axis_index("branch")
    half = lax.axis_index("zh")
    core = lax.axis_index("core")
    tok_count, width = tokens.shape
    cap = min(tok_count, 4 * tok_count // experts)
    group = 2 * cap

    wanted = jnp.stack([expert, (expert + experts // 2) % experts])
    chosen, _, slot = route_tables(routes, route_weights, wanted)
    rows = jnp.arange(group, dtype=jnp.int32)
    picks = (
        chosen.T[:, None, :]
        & (slot.T[:, None, :] == (rows % cap)[None, :, None])
        & (rows // cap == half)[None, :, None]
    ).astype(BF16)
    packed = jnp.dot(
        picks.reshape(2 * group, tok_count), tokens, preferred_element_type=F32
    ).astype(BF16)
    swap = [
        (2 * e + z, 2 * ((e + experts // 2) % experts) + 1 - z)
        for e in range(experts)
        for z in range(2)
    ]
    arrived = lax.ppermute(packed[group:], ZLINE, swap)
    both = packed[:group] + arrived
    spread = jnp.broadcast_to(both[None], (n_xy, group, width))
    mine = lax.all_to_all(spread, XY, 0, 0, tiled=True).reshape(n_xy * group, width)
    theirs = lax.ppermute(mine, "core", FLIP)

    kv, gain, _ = lax.optimization_barrier((keyval_weights[0], norm_gains, packed))
    kv_rows = kv.shape[0]
    gain_hi = lax.reduce_precision(gain, 8, 7)
    gain_lo = lax.reduce_precision(gain - gain_hi, 8, 7)
    gain_pair = jnp.concatenate([gain_hi, gain_lo], axis=0).astype(BF16)
    acc = kv
    gain_sum = None
    step = experts // 2
    while step:
        span = acc.shape[1] // 2
        upper = (expert // step) % 2 == 1
        stay = jnp.where(upper, acc[:, span:], acc[:, :span])
        leave = jnp.where(upper, acc[:, :span], acc[:, span:])
        extra = (gain_pair if gain_sum is None else gain_sum).reshape(-1, span)
        turn = [(e, e ^ step) for e in range(experts)]
        came = lax.ppermute(jnp.concatenate([leave, extra], axis=0), "branch", turn)
        came, _ = lax.optimization_barrier((came, spread))
        came = came.astype(F32)
        acc = stay.astype(F32) + came[:kv_rows]
        other = came[kv_rows:].reshape(-1, width)
        if gain_sum is None:
            gain_sum = gain + jnp.sum(other, axis=0, keepdims=True)
        else:
            gain_sum = gain_sum + other
        step //= 2
    merged_keyval = (acc / experts).astype(BF16)
    gain_avg = gain_sum[0] / experts

    def hidden_of(block):
        widened = block.astype(F32)
        inv_rms = lax.rsqrt(jnp.mean(widened * widened, axis=1, keepdims=True) + 1e-05)
        normed = (widened * inv_rms * gain_avg[None, :]).astype(BF16)
        gate = jnp.dot(normed, expert_gate[0], preferred_element_type=F32)
        up = jnp.dot(normed, expert_up[0], preferred_element_type=F32)
        return (jax.nn.silu(gate) * up).astype(BF16)

    hid_mine, hid_theirs = hidden_of(mine), hidden_of(theirs)
    units = hid_mine.shape[1]
    hid = jnp.stack(
        [
            jnp.where(core == 0, hid_mine, hid_theirs).reshape(n_xy, group, units),
            jnp.where(core == 0, hid_theirs, hid_mine).reshape(n_xy, group, units),
        ],
        axis=1,
    ).reshape(2 * n_xy * group, units)
    hid_far = lax.ppermute(hid, "zh", FLIP)
    hid = jnp.concatenate(
        [jnp.where(half == 0, hid, hid_far), jnp.where(half == 0, hid_far, hid)], axis=1
    )
    hid = lax.all_gather(hid, "core", axis=0, tiled=False)
    hid = jnp.concatenate(
        [hid[0, :, :units], hid[1, :, :units], hid[0, :, units:], hid[1, :, units:]], axis=1
    )

    down, _ = lax.optimization_barrier((expert_down[0].T, spread))
    cols = down.shape[0]
    down = split_columns(down, n_xy)
    down = lax.all_to_all(down, XY, 0, 0, tiled=True).reshape(n_xy * cols, 4 * units)
    part = lax.dot_general(
        hid, down, (((1,), (1,)), ((), ())), preferred_element_type=F32
    ).astype(BF16)
    part = part.reshape(n_xy, 2 * group, n_xy * cols)
    part = lax.all_to_all(part, XY, 0, 0, tiled=True)
    total = jnp.sum(part.astype(F32), axis=0).astype(BF16)
    keep = jnp.where(core == 0, total[:group], total[group:])
    give = jnp.where(core == 0, total[group:], total[:group])
    got = lax.ppermute(give, "core", FLIP)
    whole = jnp.stack(
        [
            jnp.where(core == 0, keep, got).reshape(2, cap, n_xy, cols),
            jnp.where(core == 0, got, keep).reshape(2, cap, n_xy, cols),
        ],
        axis=3,
    ).reshape(2, cap, n_xy * 2 * cols)
    spread = jnp.broadcast_to(whole[None], (experts,) + whole.shape)
    spread = spread.reshape((2 * experts,) + whole.shape[1:])
    slots = lax.all_to_all(spread, ZLINE, 0, 0, tiled=True)
    slots = slots.reshape((experts, 2) + whole.shape[1:])

    chosen, share, slot = route_tables(routes, route_weights, jnp.arange(experts))
    mix = jnp.where(
        chosen[:, :, None] & (slot[:, :, None] == jnp.arange(cap)), share[:, :, None], 0.0
    )
    moe = jnp.einsum(
        "tes,ezsc->tzc", mix, slots.astype(F32), precision=lax.Precision.HIGHEST
    )
    moe = moe.reshape(tok_count, 2, n_xy, 2 * cols).swapaxes(1, 2).reshape(tok_count, width)
    mixed = (tokens.astype(F32) + moe).astype(BF16)
    return mixed, merged_keyval


def solution(mesh):
    n_x = n_y = int(round((mesh.devices.shape[1] // 4) ** 0.5))
    fine = Mesh(
        mesh.devices.reshape(mesh.devices.shape[0], n_x, n_y, 2, 2),
        ("branch", "x", "y", "zh", "core"),
    )
    in_specs = (
        P(DP, None),
        P(DP, None),
        P(DP, None),
        P("branch", None),
        P("branch", DP, None),
        P("branch", None, DP),
        P("branch", None, DP),
        P("branch", None, DP),
    )
    out_specs = (P(DP, None), P(DP, "branch"))
    return jax.shard_map(layer, mesh=fine, in_specs=in_specs, out_specs=out_specs, check_vma=False)
```

```python
import functools

import jax
import jax.numpy as jnp
from jax import lax
from jax.experimental import pallas as pl
from jax.experimental.pallas import tpu as pltpu
from jax.sharding import Mesh, PartitionSpec as P

F32 = jnp.float32
BF16 = jnp.bfloat16
XY = ("x", "y")
ZLINE = ("branch", "zh")
DP = ("x", "y", "zh", "core")
FLIP = [(0, 1), (1, 0)]


def split_kernel(parts, source, target):
    span = source.shape[1] // parts
    for part in range(parts):
        target[part] = source[:, part * span : (part + 1) * span]


def split_columns(array, parts):
    rows, cols = array.shape
    return pl.pallas_call(
        functools.partial(split_kernel, parts),
        out_shape=jax.ShapeDtypeStruct((parts, rows, cols // parts), array.dtype),
        cost_estimate=pl.CostEstimate(
            flops=0, bytes_accessed=4 * rows * cols, transcendentals=0
        ),
        compiler_params=pltpu.CompilerParams(vmem_limit_bytes=8 << 20),
        name="split_columns",
    )(array)


def route_tables(routes, route_weights, experts):
    matched = routes[:, :, None] == experts[None, None, :]
    chosen = jnp.any(matched, axis=1)
    share = jnp.sum(jnp.where(matched, route_weights[:, :, None], 0.0), axis=1)
    slot = jnp.cumsum(chosen.astype(jnp.int32), axis=0) - 1
    return chosen, share, slot


def layer(
    tokens, routes, route_weights, norm_gains, keyval_weights, expert_gate, expert_up, expert_down
):
    experts = lax.axis_size("branch")
    n_xy = lax.axis_size("x") * lax.axis_size("y")
    expert = lax.axis_index("branch")
    half = lax.axis_index("zh")
    core = lax.axis_index("core")
    tok_count, width = tokens.shape
    cap = min(tok_count, 4 * tok_count // experts)
    group = 2 * cap
    steps = [experts >> shift for shift in range(1, experts.bit_length())]

    down = expert_down[0].T
    cols = down.shape[0]
    down = split_columns(down, n_xy)
    down = lax.all_to_all(down, XY, 0, 0, tiled=True).reshape(n_xy * cols, -1)

    wanted = jnp.stack([expert, (expert + experts // 2) % experts])
    chosen, _, slot = route_tables(routes, route_weights, wanted)
    rows = jnp.arange(group, dtype=jnp.int32)
    picks = (
        chosen.T[:, None, :]
        & (slot.T[:, None, :] == (rows % cap)[None, :, None])
        & (rows // cap == half)[None, :, None]
    ).astype(BF16)
    packed = jnp.dot(
        picks.reshape(2 * group, tok_count), tokens, preferred_element_type=F32
    ).astype(BF16)
    swap = [
        (2 * e + z, 2 * ((e + experts // 2) % experts) + 1 - z)
        for e in range(experts)
        for z in range(2)
    ]
    arrived = lax.ppermute(packed[group:], ZLINE, swap)
    both = packed[:group] + arrived
    spread = jnp.broadcast_to(both[None], (n_xy, group, width))
    spread, down = lax.optimization_barrier((spread, down))
    mine = lax.all_to_all(spread, XY, 0, 0, tiled=True).reshape(n_xy * group, width)
    theirs = lax.ppermute(mine, "core", FLIP)

    gain_sum = norm_gains
    for step in steps:
        turn = [(e, e ^ step) for e in range(experts)]
        came = lax.ppermute(gain_sum, "branch", turn)
        if step == steps[0]:
            came, _ = lax.optimization_barrier((came, spread))
        gain_sum = gain_sum + came
    gain_avg = gain_sum[0] / experts

    def hidden_of(block):
        widened = block.astype(F32)
        inv_rms = lax.rsqrt(jnp.mean(widened * widened, axis=1, keepdims=True) + 1e-05)
        normed = (widened * inv_rms * gain_avg[None, :]).astype(BF16)
        gate = jnp.dot(normed, expert_gate[0], preferred_element_type=F32)
        up = jnp.dot(normed, expert_up[0], preferred_element_type=F32)
        return (jax.nn.silu(gate) * up).astype(BF16)

    hid_mine, hid_theirs = hidden_of(mine), hidden_of(theirs)
    units = hid_mine.shape[1]
    hid = jnp.stack(
        [
            jnp.where(core == 0, hid_mine, hid_theirs).reshape(n_xy, group, units),
            jnp.where(core == 0, hid_theirs, hid_mine).reshape(n_xy, group, units),
        ],
        axis=1,
    ).reshape(2 * n_xy * group, units)
    hid_far = lax.ppermute(hid, "zh", FLIP)
    hid = jnp.concatenate(
        [jnp.where(half == 0, hid, hid_far), jnp.where(half == 0, hid_far, hid)], axis=1
    )
    hid = lax.all_gather(hid, "core", axis=0, tiled=False)
    hid = jnp.concatenate(
        [hid[0, :, :units], hid[1, :, :units], hid[0, :, units:], hid[1, :, units:]], axis=1
    )

    part = lax.dot_general(
        hid, down, (((1,), (1,)), ((), ())), preferred_element_type=F32
    ).astype(BF16)
    part = part.reshape(n_xy, 2 * group, n_xy * cols)

    acc, _ = lax.optimization_barrier((keyval_weights[0], hid_mine))
    for step in steps:
        span = acc.shape[1] // 2
        upper = (expert // step) % 2 == 1
        stay = jnp.where(upper, acc[:, span:], acc[:, :span])
        leave = jnp.where(upper, acc[:, :span], acc[:, span:])
        turn = [(e, e ^ step) for e in range(experts)]
        came = lax.ppermute(leave, "branch", turn)
        if step == steps[0]:
            came, _ = lax.optimization_barrier((came, part))
        acc = stay.astype(F32) + came.astype(F32)
    part = lax.all_to_all(part, XY, 0, 0, tiled=True)
    total = jnp.sum(part.astype(F32), axis=0).astype(BF16)
    keep = jnp.where(core == 0, total[:group], total[group:])
    give = jnp.where(core == 0, total[group:], total[:group])
    got = lax.ppermute(give, "core", FLIP)
    whole = jnp.stack(
        [
            jnp.where(core == 0, keep, got).reshape(2, cap, n_xy, cols),
            jnp.where(core == 0, got, keep).reshape(2, cap, n_xy, cols),
        ],
        axis=3,
    ).reshape(2, cap, n_xy * 2 * cols)
    spread = jnp.broadcast_to(whole[None], (experts,) + whole.shape)
    spread = spread.reshape((2 * experts,) + whole.shape[1:])
    acc, _ = lax.optimization_barrier((acc, spread))
    merged_keyval = (acc / experts).astype(BF16)
    slots = lax.all_to_all(spread, ZLINE, 0, 0, tiled=True)
    slots = slots.reshape((experts, 2) + whole.shape[1:])

    chosen, share, slot = route_tables(routes, route_weights, jnp.arange(experts))
    mix = jnp.where(
        chosen[:, :, None] & (slot[:, :, None] == jnp.arange(cap)), share[:, :, None], 0.0
    )
    moe = jnp.einsum(
        "tes,ezsc->tzc", mix, slots.astype(F32), precision=lax.Precision.HIGHEST
    )
    moe = moe.reshape(tok_count, 2, n_xy, 2 * cols).swapaxes(1, 2).reshape(tok_count, width)
    mixed = (tokens.astype(F32) + moe).astype(BF16)
    return mixed, merged_keyval


def solution(mesh):
    n_x = n_y = int(round((mesh.devices.shape[1] // 4) ** 0.5))
    fine = Mesh(
        mesh.devices.reshape(mesh.devices.shape[0], n_x, n_y, 2, 2),
        ("branch", "x", "y", "zh", "core"),
    )
    in_specs = (
        P(DP, None),
        P(DP, None),
        P(DP, None),
        P("branch", None),
        P("branch", DP, None),
        P("branch", None, DP),
        P("branch", None, DP),
        P("branch", None, DP),
    )
    out_specs = (P(DP, None), P(DP, "branch"))
    return jax.shard_map(layer, mesh=fine, in_specs=in_specs, out_specs=out_specs, check_vma=False)
```

```python
import functools

import jax
import jax.numpy as jnp
from jax import lax
from jax.experimental import pallas as pl
from jax.experimental.pallas import tpu as pltpu
from jax.sharding import Mesh, PartitionSpec as P

F32 = jnp.float32
BF16 = jnp.bfloat16
XY = ("x", "y")
ZLINE = ("branch", "zh")
DP = ("x", "y", "zh", "core")
FLIP = [(0, 1), (1, 0)]


def split_kernel(parts, source, target):
    span = source.shape[1] // parts
    for part in range(parts):
        target[part] = source[:, part * span : (part + 1) * span]


def split_columns(array, parts):
    rows, cols = array.shape
    return pl.pallas_call(
        functools.partial(split_kernel, parts),
        out_shape=jax.ShapeDtypeStruct((parts, rows, cols // parts), array.dtype),
        cost_estimate=pl.CostEstimate(
            flops=0, bytes_accessed=4 * rows * cols, transcendentals=0
        ),
        compiler_params=pltpu.CompilerParams(vmem_limit_bytes=8 << 20),
        name="split_columns",
    )(array)


def pick_table(route_pair, wanted, wanted_slot):
    chosen = (route_pair[0:1, :] == wanted) | (route_pair[1:2, :] == wanted)
    toks = route_pair.shape[1]
    earlier = (
        lax.broadcasted_iota(jnp.int32, (toks, toks), 0)
        <= lax.broadcasted_iota(jnp.int32, (toks, toks), 1)
    ).astype(F32)
    count = jnp.dot(chosen.astype(F32), earlier, preferred_element_type=F32)
    return chosen & (count == (wanted_slot + 1).astype(F32))


def pack_kernel(experts, cap, tokens, route_pair, own, send):
    group = 2 * cap
    toks = tokens.shape[0]
    expert = lax.axis_index("branch")
    half = lax.axis_index("zh")
    row = lax.broadcasted_iota(jnp.int32, (2 * group, toks), 0)
    wanted = jnp.where(row < group, expert, lax.rem(expert + experts // 2, experts))
    here = (row >= group) | (row // cap == half)
    picks = pick_table(route_pair[...], wanted, lax.rem(row, cap)) & here
    packed = jnp.dot(picks.astype(BF16), tokens[...], preferred_element_type=F32)
    own[...] = packed[:group].astype(BF16)
    send[...] = packed[group : group + cap].astype(BF16)


def pack_rows(experts, cap, tokens, route_pair):
    group, width = 2 * cap, tokens.shape[1]
    return pl.pallas_call(
        functools.partial(pack_kernel, experts, cap),
        out_shape=(
            jax.ShapeDtypeStruct((group, width), BF16),
            jax.ShapeDtypeStruct((cap, width), BF16),
        ),
        cost_estimate=pl.CostEstimate(flops=1 << 20, bytes_accessed=1 << 18, transcendentals=0),
        compiler_params=pltpu.CompilerParams(vmem_limit_bytes=8 << 20),
        name="pack_rows",
    )(tokens, route_pair)


def hidden_kernel(inv_width, experts, mine, theirs, gain, gate, up, hidden, sums, gates, ups):
    step = pl.program_id(0)
    rows = mine.shape[0]

    @pl.when(step == 0)
    def _():
        sums[...] = jnp.zeros_like(sums)
        gates[...] = jnp.zeros_like(gates)
        ups[...] = jnp.zeros_like(ups)

    scale = gain[...] * (1.0 / experts)
    block = jnp.concatenate([mine[...], theirs[...]], axis=0).astype(F32)
    sums[...] += jnp.sum(block * block, axis=1, keepdims=True)
    scaled = (block * scale).astype(BF16)
    gates[...] += jnp.dot(scaled, gate[...], preferred_element_type=F32)
    ups[...] += jnp.dot(scaled, up[...], preferred_element_type=F32)

    @pl.when(step == pl.num_programs(0) - 1)
    def _():
        core = lax.axis_index("core")
        inv_rms = lax.rsqrt(sums[...] * inv_width + 1e-05)
        gate_part = gates[...] * inv_rms
        value = gate_part / (1.0 + jnp.exp(-gate_part)) * (ups[...] * inv_rms)
        value = value.astype(BF16)
        shape = (hidden.shape[0], hidden.shape[2], hidden.shape[3])
        hidden[:, core] = value[:rows].reshape(shape)
        hidden[:, 1 - core] = value[rows:].reshape(shape)


def hidden_units(experts, n_xy, mine, theirs, gain, gate, up, parts=4):
    rows, width = mine.shape
    units = gate.shape[1]
    span = width // parts
    return pl.pallas_call(
        functools.partial(hidden_kernel, 1.0 / width, experts),
        out_shape=jax.ShapeDtypeStruct((n_xy, 2, rows // n_xy, units), BF16),
        grid=(parts,),
        in_specs=[
            pl.BlockSpec((rows, span), lambda k: (0, k)),
            pl.BlockSpec((rows, span), lambda k: (0, k)),
            pl.BlockSpec((1, span), lambda k: (0, k)),
            pl.BlockSpec((span, units), lambda k: (k, 0)),
            pl.BlockSpec((span, units), lambda k: (k, 0)),
        ],
        out_specs=pl.BlockSpec((n_xy, 2, rows // n_xy, units), lambda k: (0, 0, 0, 0)),
        scratch_shapes=[
            pltpu.VMEM((2 * rows, 1), F32),
            pltpu.VMEM((2 * rows, units), F32),
            pltpu.VMEM((2 * rows, units), F32),
        ],
        cost_estimate=pl.CostEstimate(
            flops=8 * rows * width * units, bytes_accessed=1 << 22, transcendentals=1 << 16
        ),
        compiler_params=pltpu.CompilerParams(
            dimension_semantics=("arbitrary",), vmem_limit_bytes=8 << 20
        ),
        name="hidden_units",
    )(mine, theirs, gain, gate, up)


def fan_kernel(cap, total, fan):
    core = lax.axis_index("core")
    group = 2 * cap
    start = pl.multiple_of(core * group, group)
    left = total[0, pl.ds(start, group), :].astype(F32)
    right = total[1, pl.ds(start, group), :].astype(F32)
    line = lax.broadcasted_iota(jnp.int32, left.shape, 0)
    low = jnp.where(line < cap, left, pltpu.roll(right, cap, 0)).astype(BF16)
    high = jnp.where(line < cap, pltpu.roll(left, cap, 0), right).astype(BF16)
    for place in range(fan.shape[0] // 2):
        fan[2 * place] = low
        fan[2 * place + 1] = high


def fan_out(experts, cap, total):
    return pl.pallas_call(
        functools.partial(fan_kernel, cap),
        out_shape=jax.ShapeDtypeStruct((2 * experts, 2 * cap, total.shape[2]), BF16),
        cost_estimate=pl.CostEstimate(flops=1 << 16, bytes_accessed=1 << 19, transcendentals=0),
        compiler_params=pltpu.CompilerParams(vmem_limit_bytes=8 << 20),
        name="fan_out",
    )(total)


def mix_kernel(experts, cap, cols, tokens, route_pair, weight_pair, slots, mixed):
    toks = tokens.shape[0]
    group = 2 * cap
    keys = experts * group
    row = lax.broadcasted_iota(jnp.int32, (keys, toks), 0)
    wanted = row // group
    pair = route_pair[...]
    weights = weight_pair[...]
    picks = pick_table(pair, wanted, lax.rem(row, cap))
    share = jnp.where(pair[0:1, :] == wanted, weights[0:1, :], 0.0) + jnp.where(
        pair[1:2, :] == wanted, weights[1:2, :], 0.0
    )
    share = jnp.where(picks, share, 0.0)
    side = lax.rem(row // cap, 2)
    span = slots.shape[3]
    for half in range(2):
        rows = slots[:, half].astype(F32).reshape(keys, span)
        parts = [
            lax.dot_general(
                jnp.where(side == core, share, 0.0),
                rows,
                (((0,), (0,)), ((), ())),
                precision=lax.Precision.HIGHEST,
                preferred_element_type=F32,
            )
            for core in range(2)
        ]
        for block in range(span // cols):
            base = (block * 4 + half * 2) * cols
            cut = slice(block * cols, (block + 1) * cols)
            moe = jnp.concatenate([parts[0][:, cut], parts[1][:, cut]], axis=1)
            place = slice(base, base + 2 * cols)
            mixed[:, place] = (tokens[:, place].astype(F32) + moe).astype(BF16)


def mix_tokens(experts, cap, cols, tokens, route_pair, weight_pair, slots):
    return pl.pallas_call(
        functools.partial(mix_kernel, experts, cap, cols),
        out_shape=jax.ShapeDtypeStruct(tokens.shape, BF16),
        cost_estimate=pl.CostEstimate(flops=1 << 24, bytes_accessed=1 << 19, transcendentals=0),
        compiler_params=pltpu.CompilerParams(vmem_limit_bytes=8 << 20),
        name="mix_tokens",
    )(tokens, route_pair, weight_pair, slots)


def layer(
    tokens, routes, route_weights, norm_gains, keyval_weights, expert_gate, expert_up, expert_down
):
    experts = lax.axis_size("branch")
    n_xy = lax.axis_size("x") * lax.axis_size("y")
    expert = lax.axis_index("branch")
    half = lax.axis_index("zh")
    tok_count, width = tokens.shape
    cap = min(tok_count, 4 * tok_count // experts)
    group = 2 * cap
    steps = [experts >> shift for shift in range(1, experts.bit_length())]

    route_pair, weight_pair = routes.T, route_weights.T
    own, send = pack_rows(experts, cap, tokens, route_pair)
    swap = [
        (2 * e + z, 2 * ((e + experts // 2) % experts) + 1 - z)
        for e in range(experts)
        for z in range(2)
    ]
    arrived = lax.ppermute(send, ZLINE, swap)
    line = lax.broadcasted_iota(jnp.int32, own.shape, 0)
    both = jnp.where(line // cap == half, own, jnp.concatenate([arrived, arrived], axis=0))
    spread = jnp.broadcast_to(both[None], (n_xy, group, width))
    mine = lax.all_to_all(spread, XY, 0, 0, tiled=True).reshape(n_xy * group, width)
    theirs = lax.ppermute(mine, "core", FLIP)

    gain_sum = norm_gains
    for step in steps:
        came = lax.ppermute(gain_sum, "branch", [(b, b ^ step) for b in range(experts)])
        if step == steps[0]:
            came, _ = lax.optimization_barrier((came, spread))
        gain_sum = gain_sum + came

    down, _ = lax.optimization_barrier((expert_down[0].T, spread))
    cols = down.shape[0]
    down = split_columns(down, n_xy)
    down = lax.all_to_all(down, XY, 0, 0, tiled=True).reshape(n_xy * cols, -1)

    hid = hidden_units(experts, n_xy, mine, theirs, gain_sum, expert_gate[0], expert_up[0])
    units = hid.shape[3]
    hid = hid.reshape(2 * n_xy * group, units)
    hid_far = lax.ppermute(hid, "zh", FLIP)
    near = jnp.concatenate(
        [jnp.where(half == 0, hid, hid_far), jnp.where(half == 0, hid_far, hid)], axis=1
    )
    near = lax.all_gather(near, "core", axis=0, tiled=False)
    near = jnp.concatenate(
        [near[0, :, :units], near[1, :, :units], near[0, :, units:], near[1, :, units:]], axis=1
    )

    part = lax.dot_general(
        near, down, (((1,), (1,)), ((), ())), preferred_element_type=F32
    ).astype(BF16)
    part = part.reshape(n_xy, 2 * group, n_xy * cols)

    acc, _ = lax.optimization_barrier((keyval_weights[0], send))
    until = dict(zip(steps, (hid, part, part)))
    for step in steps:
        span = acc.shape[1] // 2
        upper = (expert // step) % 2 == 1
        stay = jnp.where(upper, acc[:, span:], acc[:, :span])
        leave = jnp.where(upper, acc[:, :span], acc[:, span:])
        came = lax.ppermute(leave, "branch", [(b, b ^ step) for b in range(experts)])
        came, _ = lax.optimization_barrier((came, until[step]))
        acc = stay.astype(F32) + came.astype(F32)

    part = lax.all_to_all(part, XY, 0, 0, tiled=True)
    total = jnp.sum(part.astype(F32), axis=0).astype(BF16)
    total = lax.all_gather(total, "core", axis=0, tiled=False)
    spread = fan_out(experts, cap, total)
    slots = lax.all_to_all(spread, ZLINE, 0, 0, tiled=True)
    slots = slots.reshape(experts, 2, group, n_xy * cols)
    acc, _ = lax.optimization_barrier((acc, spread))
    merged_keyval = (acc / experts).astype(BF16)
    mixed = mix_tokens(experts, cap, cols, tokens, route_pair, weight_pair, slots)
    return mixed, merged_keyval


def solution(mesh):
    n_x = n_y = int(round((mesh.devices.shape[1] // 4) ** 0.5))
    fine = Mesh(
        mesh.devices.reshape(mesh.devices.shape[0], n_x, n_y, 2, 2),
        ("branch", "x", "y", "zh", "core"),
    )
    in_specs = (
        P(DP, None),
        P(DP, None),
        P(DP, None),
        P("branch", None),
        P("branch", DP, None),
        P("branch", None, DP),
        P("branch", None, DP),
        P("branch", None, DP),
    )
    out_specs = (P(DP, None), P(DP, "branch"))
    return jax.shard_map(layer, mesh=fine, in_specs=in_specs, out_specs=out_specs, check_vma=False)
```

```python
import functools

import jax
import jax.numpy as jnp
from jax import lax
from jax.experimental import pallas as pl
from jax.experimental.pallas import tpu as pltpu
from jax.sharding import Mesh, PartitionSpec as P

F32 = jnp.float32
BF16 = jnp.bfloat16
XY = ("x", "y")
ZLINE = ("branch", "zh")
DP = ("x", "y", "zh", "core")
FLIP = [(0, 1), (1, 0)]


def split_kernel(parts, source, target):
    span = source.shape[1] // parts
    for part in range(parts):
        target[part] = source[:, part * span : (part + 1) * span]


def split_columns(array, parts):
    rows, cols = array.shape
    return pl.pallas_call(
        functools.partial(split_kernel, parts),
        out_shape=jax.ShapeDtypeStruct((parts, rows, cols // parts), array.dtype),
        cost_estimate=pl.CostEstimate(
            flops=0, bytes_accessed=4 * rows * cols, transcendentals=0
        ),
        compiler_params=pltpu.CompilerParams(vmem_limit_bytes=8 << 20),
        name="split_columns",
    )(array)


def stage_kernel(parts, source, target, sems):
    span = target.shape[0] // parts
    loads = [
        pltpu.make_async_copy(
            source.at[pl.ds(part * span, span)], target.at[pl.ds(part * span, span)], sems.at[part]
        )
        for part in range(parts)
    ]
    for load in loads:
        load.start()
    for load in loads:
        load.wait()


def stage(array, parts=4):
    return pl.pallas_call(
        functools.partial(stage_kernel, parts),
        out_shape=jax.ShapeDtypeStruct(array.shape, array.dtype),
        in_specs=[pl.BlockSpec(memory_space=pltpu.HBM)],
        out_specs=pl.BlockSpec(memory_space=pltpu.VMEM),
        scratch_shapes=[pltpu.SemaphoreType.DMA((parts,))],
        cost_estimate=pl.CostEstimate(flops=0, bytes_accessed=2 * array.size, transcendentals=0),
        compiler_params=pltpu.CompilerParams(vmem_limit_bytes=4 << 20),
        name="stage",
    )(array)


def pick_table(route_pair, wanted, wanted_slot):
    chosen = (route_pair[0:1, :] == wanted) | (route_pair[1:2, :] == wanted)
    toks = route_pair.shape[1]
    earlier = (
        lax.broadcasted_iota(jnp.int32, (toks, toks), 0)
        <= lax.broadcasted_iota(jnp.int32, (toks, toks), 1)
    ).astype(F32)
    count = jnp.dot(chosen.astype(F32), earlier, preferred_element_type=F32)
    return chosen & (count == (wanted_slot + 1).astype(F32))


def pack_kernel(experts, cap, tokens, route_pair, own, send):
    group = 2 * cap
    toks = tokens.shape[0]
    expert = lax.axis_index("branch")
    half = lax.axis_index("zh")
    row = lax.broadcasted_iota(jnp.int32, (2 * group, toks), 0)
    wanted = jnp.where(row < group, expert, lax.rem(expert + experts // 2, experts))
    here = (row >= group) | (row // cap == half)
    picks = pick_table(route_pair[...], wanted, lax.rem(row, cap)) & here
    packed = jnp.dot(picks.astype(BF16), tokens[...], preferred_element_type=F32)
    own[...] = packed[:group].astype(BF16)
    send[...] = packed[group : group + cap].astype(BF16)


def pack_rows(experts, cap, tokens, route_pair):
    group, width = 2 * cap, tokens.shape[1]
    return pl.pallas_call(
        functools.partial(pack_kernel, experts, cap),
        out_shape=(
            jax.ShapeDtypeStruct((group, width), BF16),
            jax.ShapeDtypeStruct((cap, width), BF16),
        ),
        cost_estimate=pl.CostEstimate(flops=1 << 20, bytes_accessed=1 << 18, transcendentals=0),
        compiler_params=pltpu.CompilerParams(vmem_limit_bytes=8 << 20),
        name="pack_rows",
    )(tokens, route_pair)


def hidden_kernel(experts, parts, mine, theirs_hbm, gain, gate, up, hidden, theirs, sems):
    _, width = mine.shape
    span = width // parts
    cuts = [slice(part * span, (part + 1) * span) for part in range(parts)]
    loads = [
        pltpu.make_async_copy(theirs_hbm.at[:, cut], theirs.at[:, cut], sems.at[part])
        for part, cut in enumerate(cuts)
    ]
    for load in loads:
        load.start()
    sides = []
    for source, waits in ((mine, ()), (theirs, loads)):
        gate_part = up_part = total = None
        for part, cut in enumerate(cuts):
            if waits:
                waits[part].wait()
            scale = gain[:, cut] * (1.0 / experts)
            block = source[:, cut].astype(F32)
            square = jnp.sum(block * block, axis=1, keepdims=True)
            scaled = (block * scale).astype(BF16)
            gates = jnp.dot(scaled, gate[cut, :], preferred_element_type=F32)
            ups = jnp.dot(scaled, up[cut, :], preferred_element_type=F32)
            total = square if total is None else total + square
            gate_part = gates if gate_part is None else gate_part + gates
            up_part = ups if up_part is None else up_part + ups
        inv_rms = lax.rsqrt(total * (1.0 / width) + 1e-05)
        gate_part = gate_part * inv_rms
        value = gate_part / (1.0 + jnp.exp(-gate_part)) * (up_part * inv_rms)
        sides.append(value.astype(BF16))
    core = lax.axis_index("core")
    shape = (hidden.shape[0], hidden.shape[2], hidden.shape[3])
    hidden[:, core] = sides[0].reshape(shape)
    hidden[:, 1 - core] = sides[1].reshape(shape)


def hidden_units(experts, n_xy, mine, theirs, gain, gate, up, parts=4):
    rows, width = mine.shape
    units = gate.shape[1]
    whole = pl.BlockSpec(memory_space=pltpu.VMEM)
    return pl.pallas_call(
        functools.partial(hidden_kernel, experts, parts),
        out_shape=jax.ShapeDtypeStruct((n_xy, 2, rows // n_xy, units), BF16),
        in_specs=[whole, pl.BlockSpec(memory_space=pltpu.HBM), whole, whole, whole],
        out_specs=whole,
        scratch_shapes=[
            pltpu.VMEM(theirs.shape, theirs.dtype),
            pltpu.SemaphoreType.DMA((parts,)),
        ],
        cost_estimate=pl.CostEstimate(
            flops=8 * rows * width * units, bytes_accessed=1 << 22, transcendentals=1 << 16
        ),
        compiler_params=pltpu.CompilerParams(vmem_limit_bytes=8 << 20),
        name="hidden_units",
    )(mine, theirs, gain, gate, up)


def fan_kernel(cap, total, fan):
    core = lax.axis_index("core")
    group = 2 * cap
    start = pl.multiple_of(core * group, group)
    left = total[0, pl.ds(start, group), :].astype(F32)
    right = total[1, pl.ds(start, group), :].astype(F32)
    line = lax.broadcasted_iota(jnp.int32, left.shape, 0)
    low = jnp.where(line < cap, left, pltpu.roll(right, cap, 0)).astype(BF16)
    high = jnp.where(line < cap, pltpu.roll(left, cap, 0), right).astype(BF16)
    for place in range(fan.shape[0] // 2):
        fan[2 * place] = low
        fan[2 * place + 1] = high


def fan_out(experts, cap, total):
    return pl.pallas_call(
        functools.partial(fan_kernel, cap),
        out_shape=jax.ShapeDtypeStruct((2 * experts, 2 * cap, total.shape[2]), BF16),
        cost_estimate=pl.CostEstimate(flops=1 << 16, bytes_accessed=1 << 19, transcendentals=0),
        compiler_params=pltpu.CompilerParams(vmem_limit_bytes=8 << 20),
        name="fan_out",
    )(total)


def table_kernel(experts, cap, tokens, route_pair, weight_pair, table, widened):
    toks = tokens.shape[0]
    group = 2 * cap
    row = lax.broadcasted_iota(jnp.int32, (experts * group, toks), 0)
    wanted = row // group
    pair = route_pair[...]
    weights = weight_pair[...]
    picks = pick_table(pair, wanted, lax.rem(row, cap))
    share = jnp.where(pair[0:1, :] == wanted, weights[0:1, :], 0.0) + jnp.where(
        pair[1:2, :] == wanted, weights[1:2, :], 0.0
    )
    share = jnp.where(picks, share, 0.0)
    side = lax.rem(row // cap, 2)
    for core in range(2):
        table[core] = jnp.where(side == core, share, 0.0)
    widened[...] = tokens[...].astype(F32)


def mix_table(experts, cap, tokens, route_pair, weight_pair):
    keys = experts * 2 * cap
    return pl.pallas_call(
        functools.partial(table_kernel, experts, cap),
        out_shape=(
            jax.ShapeDtypeStruct((2, keys, tokens.shape[0]), F32),
            jax.ShapeDtypeStruct(tokens.shape, F32),
        ),
        cost_estimate=pl.CostEstimate(flops=1 << 18, bytes_accessed=1 << 18, transcendentals=0),
        compiler_params=pltpu.CompilerParams(vmem_limit_bytes=8 << 20),
        name="mix_table",
    )(tokens, route_pair, weight_pair)


def mix_kernel(cols, table, widened, slots, mixed):
    keys, span = table.shape[1], slots.shape[3]
    for half in range(2):
        rows = slots[:, half].astype(F32).reshape(keys, span)
        parts = [
            lax.dot_general(
                table[core],
                rows,
                (((0,), (0,)), ((), ())),
                precision=lax.Precision.HIGHEST,
                preferred_element_type=F32,
            )
            for core in range(2)
        ]
        for block in range(span // cols):
            base = (block * 4 + half * 2) * cols
            cut = slice(block * cols, (block + 1) * cols)
            moe = jnp.concatenate([parts[0][:, cut], parts[1][:, cut]], axis=1)
            place = slice(base, base + 2 * cols)
            mixed[:, place] = (widened[:, place] + moe).astype(BF16)


def mix_tokens(cols, table, widened, slots):
    return pl.pallas_call(
        functools.partial(mix_kernel, cols),
        out_shape=jax.ShapeDtypeStruct(widened.shape, BF16),
        cost_estimate=pl.CostEstimate(flops=1 << 24, bytes_accessed=1 << 19, transcendentals=0),
        compiler_params=pltpu.CompilerParams(vmem_limit_bytes=8 << 20),
        name="mix_tokens",
    )(table, widened, slots)


def layer(
    tokens, routes, route_weights, norm_gains, keyval_weights, expert_gate, expert_up, expert_down
):
    experts = lax.axis_size("branch")
    n_xy = lax.axis_size("x") * lax.axis_size("y")
    expert = lax.axis_index("branch")
    half = lax.axis_index("zh")
    tok_count, width = tokens.shape
    cap = min(tok_count, 4 * tok_count // experts)
    group = 2 * cap
    steps = [experts >> shift for shift in range(1, experts.bit_length())]

    route_pair, weight_pair = routes.T, route_weights.T
    own, send = pack_rows(experts, cap, tokens, route_pair)
    swap = [
        (2 * e + z, 2 * ((e + experts // 2) % experts) + 1 - z)
        for e in range(experts)
        for z in range(2)
    ]
    arrived = lax.ppermute(send, ZLINE, swap)
    line = lax.broadcasted_iota(jnp.int32, own.shape, 0)
    both = jnp.where(line // cap == half, own, jnp.concatenate([arrived, arrived], axis=0))
    spread = jnp.broadcast_to(both[None], (n_xy, group, width))
    mine = lax.all_to_all(spread, XY, 0, 0, tiled=True).reshape(n_xy * group, width)
    theirs = lax.ppermute(mine, "core", FLIP)

    gain_sum = norm_gains
    for step in steps:
        came = lax.ppermute(gain_sum, "branch", [(b, b ^ step) for b in range(experts)])
        if step == steps[0]:
            came, _ = lax.optimization_barrier((came, spread))
        gain_sum = gain_sum + came

    down, _ = lax.optimization_barrier((expert_down[0].T, spread))
    cols = down.shape[0]
    down = split_columns(down, n_xy)
    down = lax.all_to_all(down, XY, 0, 0, tiled=True).reshape(n_xy * cols, -1)

    gate, up, _ = lax.optimization_barrier((expert_gate[0], expert_up[0], spread))
    gate, up = stage(gate), stage(up)
    hid = hidden_units(experts, n_xy, mine, theirs, gain_sum, gate, up)
    units = hid.shape[3]
    hid = hid.reshape(2 * n_xy * group, units)
    hid_far = lax.ppermute(hid, "zh", FLIP)
    down = stage(down)
    hid_far, down = lax.optimization_barrier((hid_far, down))
    near = jnp.concatenate(
        [jnp.where(half == 0, hid, hid_far), jnp.where(half == 0, hid_far, hid)], axis=1
    )
    near = lax.all_gather(near, "core", axis=0, tiled=False)
    near = jnp.concatenate(
        [near[0, :, :units], near[1, :, :units], near[0, :, units:], near[1, :, units:]], axis=1
    )

    part = lax.dot_general(
        near, down, (((1,), (1,)), ((), ())), preferred_element_type=F32
    ).astype(BF16)
    part = part.reshape(n_xy, 2 * group, n_xy * cols)

    def halve(acc, step):
        span = acc.shape[1] // 2
        upper = (expert // step) % 2 == 1
        stay = jnp.where(upper, acc[:, span:], acc[:, :span])
        leave = jnp.where(upper, acc[:, :span], acc[:, span:])
        came = lax.ppermute(leave, "branch", [(b, b ^ step) for b in range(experts)])
        return stay, came

    def join(stay, came, after):
        came, _ = lax.optimization_barrier((came, after))
        return stay.astype(F32) + came.astype(F32)

    kv, _ = lax.optimization_barrier((keyval_weights[0], hid))
    kv = join(*halve(kv, steps[0]), part)
    kv = halve(kv, steps[1])

    part = lax.all_to_all(part, XY, 0, 0, tiled=True)
    total = jnp.sum(part.astype(F32), axis=0).astype(BF16)
    kv = join(*kv, total)
    total = lax.all_gather(total, "core", axis=0, tiled=False)
    spread = fan_out(experts, cap, total)
    kv, _ = lax.optimization_barrier((kv, spread))
    kv = join(*halve(kv, steps[2]), spread)
    slots = lax.all_to_all(spread, ZLINE, 0, 0, tiled=True)
    slots = slots.reshape(experts, 2, group, n_xy * cols)
    late_tokens, _ = lax.optimization_barrier((tokens, spread))
    merged_keyval = (kv / experts).astype(BF16)
    table, widened = mix_table(experts, cap, late_tokens, route_pair, weight_pair)
    mixed = mix_tokens(cols, table, widened, slots)
    return mixed, merged_keyval


def solution(mesh):
    n_x = n_y = int(round((mesh.devices.shape[1] // 4) ** 0.5))
    fine = Mesh(
        mesh.devices.reshape(mesh.devices.shape[0], n_x, n_y, 2, 2),
        ("branch", "x", "y", "zh", "core"),
    )
    in_specs = (
        P(DP, None),
        P(DP, None),
        P(DP, None),
        P("branch", None),
        P("branch", DP, None),
        P("branch", None, DP),
        P("branch", None, DP),
        P("branch", None, DP),
    )
    out_specs = (P(DP, None), P(DP, "branch"))
    return jax.shard_map(layer, mesh=fine, in_specs=in_specs, out_specs=out_specs, check_vma=False)
```

```python
import functools

import jax
import jax.numpy as jnp
from jax import lax
from jax.experimental import pallas as pl
from jax.experimental.pallas import tpu as pltpu
from jax.sharding import Mesh, PartitionSpec as P

F32 = jnp.float32
BF16 = jnp.bfloat16
XY = ("x", "y")
ZLINE = ("branch", "zh")
DP = ("x", "y", "zh", "core")
FLIP = [(0, 1), (1, 0)]


def split_kernel(parts, source, target):
    span = source.shape[1] // parts
    for part in range(parts):
        target[part] = source[:, part * span : (part + 1) * span]


def split_columns(array, parts):
    rows, cols = array.shape
    return pl.pallas_call(
        functools.partial(split_kernel, parts),
        out_shape=jax.ShapeDtypeStruct((parts, rows, cols // parts), array.dtype),
        cost_estimate=pl.CostEstimate(
            flops=0, bytes_accessed=4 * rows * cols, transcendentals=0
        ),
        compiler_params=pltpu.CompilerParams(vmem_limit_bytes=8 << 20),
        name="split_columns",
    )(array)


def stage_kernel(parts, source, target, sems):
    span = target.shape[0] // parts
    loads = [
        pltpu.make_async_copy(
            source.at[pl.ds(part * span, span)], target.at[pl.ds(part * span, span)], sems.at[part]
        )
        for part in range(parts)
    ]
    for load in loads:
        load.start()
    for load in loads:
        load.wait()


def stage(array, parts=4):
    return pl.pallas_call(
        functools.partial(stage_kernel, parts),
        out_shape=jax.ShapeDtypeStruct(array.shape, array.dtype),
        in_specs=[pl.BlockSpec(memory_space=pltpu.HBM)],
        out_specs=pl.BlockSpec(memory_space=pltpu.VMEM),
        scratch_shapes=[pltpu.SemaphoreType.DMA((parts,))],
        cost_estimate=pl.CostEstimate(flops=0, bytes_accessed=2 * array.size, transcendentals=0),
        compiler_params=pltpu.CompilerParams(vmem_limit_bytes=4 << 20),
        name="stage",
    )(array)


def pick_table(route_pair, wanted, wanted_slot):
    chosen = (route_pair[0:1, :] == wanted) | (route_pair[1:2, :] == wanted)
    toks = route_pair.shape[1]
    earlier = (
        lax.broadcasted_iota(jnp.int32, (toks, toks), 0)
        <= lax.broadcasted_iota(jnp.int32, (toks, toks), 1)
    ).astype(F32)
    count = jnp.dot(chosen.astype(F32), earlier, preferred_element_type=F32)
    return chosen & (count == (wanted_slot + 1).astype(F32))


def pack_kernel(experts, cap, tokens, route_pair, own, send):
    group = 2 * cap
    toks = tokens.shape[0]
    expert = lax.axis_index("branch")
    half = lax.axis_index("zh")
    row = lax.broadcasted_iota(jnp.int32, (2 * group, toks), 0)
    wanted = jnp.where(row < group, expert, lax.rem(expert + experts // 2, experts))
    here = (row >= group) | (row // cap == half)
    picks = pick_table(route_pair[...], wanted, lax.rem(row, cap)) & here
    packed = jnp.dot(picks.astype(BF16), tokens[...], preferred_element_type=F32)
    own[...] = packed[:group].astype(BF16)
    send[...] = packed[group : group + cap].astype(BF16)


def pack_rows(experts, cap, tokens, route_pair):
    group, width = 2 * cap, tokens.shape[1]
    return pl.pallas_call(
        functools.partial(pack_kernel, experts, cap),
        out_shape=(
            jax.ShapeDtypeStruct((group, width), BF16),
            jax.ShapeDtypeStruct((cap, width), BF16),
        ),
        cost_estimate=pl.CostEstimate(flops=1 << 20, bytes_accessed=1 << 18, transcendentals=0),
        compiler_params=pltpu.CompilerParams(vmem_limit_bytes=8 << 20),
        name="pack_rows",
    )(tokens, route_pair)


def hidden_kernel(experts, parts, mine, theirs_hbm, gain, gate, up, hidden, theirs, sems):
    _, width = mine.shape
    span = width // parts
    cuts = [slice(part * span, (part + 1) * span) for part in range(parts)]
    loads = [
        pltpu.make_async_copy(theirs_hbm.at[:, cut], theirs.at[:, cut], sems.at[part])
        for part, cut in enumerate(cuts)
    ]
    for load in loads:
        load.start()
    sides = []
    for source, waits in ((mine, ()), (theirs, loads)):
        gate_part = up_part = total = None
        for part, cut in enumerate(cuts):
            if waits:
                waits[part].wait()
            scale = gain[:, cut] * (1.0 / experts)
            block = source[:, cut].astype(F32)
            square = jnp.sum(block * block, axis=1, keepdims=True)
            scaled = (block * scale).astype(BF16)
            gates = jnp.dot(scaled, gate[cut, :], preferred_element_type=F32)
            ups = jnp.dot(scaled, up[cut, :], preferred_element_type=F32)
            total = square if total is None else total + square
            gate_part = gates if gate_part is None else gate_part + gates
            up_part = ups if up_part is None else up_part + ups
        inv_rms = lax.rsqrt(total * (1.0 / width) + 1e-05)
        gate_part = gate_part * inv_rms
        value = gate_part / (1.0 + jnp.exp(-gate_part)) * (up_part * inv_rms)
        sides.append(value.astype(BF16))
    core = lax.axis_index("core")
    shape = (hidden.shape[0], hidden.shape[2], hidden.shape[3])
    hidden[:, core] = sides[0].reshape(shape)
    hidden[:, 1 - core] = sides[1].reshape(shape)


def hidden_units(experts, n_xy, mine, theirs, gain, gate, up, parts=4):
    rows, width = mine.shape
    units = gate.shape[1]
    whole = pl.BlockSpec(memory_space=pltpu.VMEM)
    return pl.pallas_call(
        functools.partial(hidden_kernel, experts, parts),
        out_shape=jax.ShapeDtypeStruct((n_xy, 2, rows // n_xy, units), BF16),
        in_specs=[whole, pl.BlockSpec(memory_space=pltpu.HBM), whole, whole, whole],
        out_specs=whole,
        scratch_shapes=[
            pltpu.VMEM(theirs.shape, theirs.dtype),
            pltpu.SemaphoreType.DMA((parts,)),
        ],
        cost_estimate=pl.CostEstimate(
            flops=8 * rows * width * units, bytes_accessed=1 << 22, transcendentals=1 << 16
        ),
        compiler_params=pltpu.CompilerParams(vmem_limit_bytes=8 << 20),
        name="hidden_units",
    )(mine, theirs, gain, gate, up)


def fan_kernel(cap, total, fan):
    core = lax.axis_index("core")
    group = 2 * cap
    start = pl.multiple_of(core * group, group)
    left = total[0, pl.ds(start, group), :].astype(F32)
    right = total[1, pl.ds(start, group), :].astype(F32)
    line = lax.broadcasted_iota(jnp.int32, left.shape, 0)
    low = jnp.where(line < cap, left, pltpu.roll(right, cap, 0)).astype(BF16)
    high = jnp.where(line < cap, pltpu.roll(left, cap, 0), right).astype(BF16)
    for place in range(fan.shape[0] // 2):
        fan[2 * place] = low
        fan[2 * place + 1] = high


def fan_out(experts, cap, total):
    return pl.pallas_call(
        functools.partial(fan_kernel, cap),
        out_shape=jax.ShapeDtypeStruct((2 * experts, 2 * cap, total.shape[2]), BF16),
        cost_estimate=pl.CostEstimate(flops=1 << 16, bytes_accessed=1 << 19, transcendentals=0),
        compiler_params=pltpu.CompilerParams(vmem_limit_bytes=8 << 20),
        name="fan_out",
    )(total)


def table_kernel(experts, cap, tokens, route_pair, weight_pair, table, widened):
    toks = tokens.shape[0]
    group = 2 * cap
    row = lax.broadcasted_iota(jnp.int32, (experts * group, toks), 0)
    wanted = row // group
    pair = route_pair[...]
    weights = weight_pair[...]
    picks = pick_table(pair, wanted, lax.rem(row, cap))
    share = jnp.where(pair[0:1, :] == wanted, weights[0:1, :], 0.0) + jnp.where(
        pair[1:2, :] == wanted, weights[1:2, :], 0.0
    )
    share = jnp.where(picks, share, 0.0)
    side = lax.rem(row // cap, 2)
    terms = []
    for core in range(2):
        rest = jnp.where(side == core, share, 0.0)
        for _ in range(3):
            term = rest.astype(BF16)
            rest = rest - term.astype(F32)
            terms.append(term.astype(F32))
    table[...] = jnp.concatenate(terms, axis=1).astype(BF16)
    widened[...] = tokens[...].astype(F32)


def mix_table(experts, cap, tokens, route_pair, weight_pair):
    keys = experts * 2 * cap
    return pl.pallas_call(
        functools.partial(table_kernel, experts, cap),
        out_shape=(
            jax.ShapeDtypeStruct((keys, 6 * tokens.shape[0]), BF16),
            jax.ShapeDtypeStruct(tokens.shape, F32),
        ),
        cost_estimate=pl.CostEstimate(flops=1 << 18, bytes_accessed=1 << 18, transcendentals=0),
        compiler_params=pltpu.CompilerParams(vmem_limit_bytes=8 << 20),
        name="mix_table",
    )(tokens, route_pair, weight_pair)


def mix_kernel(cols, table, widened, slots, mixed):
    keys, span = table.shape[0], slots.shape[3]
    toks = widened.shape[0]
    for half in range(2):
        rows = slots[:, half].reshape(keys, span)
        sums = lax.dot_general(
            table[...], rows, (((0,), (0,)), ((), ())), preferred_element_type=F32
        )
        terms = [sums[toks * term : toks * (term + 1)] for term in range(6)]
        parts = [terms[3 * core] + terms[3 * core + 1] + terms[3 * core + 2] for core in range(2)]
        for block in range(span // cols):
            base = (block * 4 + half * 2) * cols
            cut = slice(block * cols, (block + 1) * cols)
            moe = jnp.concatenate([parts[0][:, cut], parts[1][:, cut]], axis=1)
            place = slice(base, base + 2 * cols)
            mixed[:, place] = (widened[:, place] + moe).astype(BF16)


def mix_tokens(cols, table, widened, slots):
    return pl.pallas_call(
        functools.partial(mix_kernel, cols),
        out_shape=jax.ShapeDtypeStruct(widened.shape, BF16),
        cost_estimate=pl.CostEstimate(flops=1 << 24, bytes_accessed=1 << 19, transcendentals=0),
        compiler_params=pltpu.CompilerParams(vmem_limit_bytes=8 << 20),
        name="mix_tokens",
    )(table, widened, slots)


def layer(
    tokens, routes, route_weights, norm_gains, keyval_weights, expert_gate, expert_up, expert_down
):
    experts = lax.axis_size("branch")
    n_xy = lax.axis_size("x") * lax.axis_size("y")
    expert = lax.axis_index("branch")
    half = lax.axis_index("zh")
    tok_count, width = tokens.shape
    cap = min(tok_count, 4 * tok_count // experts)
    group = 2 * cap
    steps = [experts >> shift for shift in range(1, experts.bit_length())]

    route_pair, weight_pair = routes.T, route_weights.T
    own, send = pack_rows(experts, cap, tokens, route_pair)
    swap = [
        (2 * e + z, 2 * ((e + experts // 2) % experts) + 1 - z)
        for e in range(experts)
        for z in range(2)
    ]
    arrived = lax.ppermute(send, ZLINE, swap)
    line = lax.broadcasted_iota(jnp.int32, own.shape, 0)
    both = jnp.where(line // cap == half, own, jnp.concatenate([arrived, arrived], axis=0))
    spread = jnp.broadcast_to(both[None], (n_xy, group, width))
    mine = lax.all_to_all(spread, XY, 0, 0, tiled=True).reshape(n_xy * group, width)
    theirs = lax.ppermute(mine, "core", FLIP)

    gain_sum = norm_gains
    for step in reversed(steps):
        came = lax.ppermute(gain_sum, "branch", [(b, b ^ step) for b in range(experts)])
        if step == steps[-1]:
            came, _ = lax.optimization_barrier((came, spread))
        gain_sum = gain_sum + came

    down, _ = lax.optimization_barrier((expert_down[0].T, spread))
    cols = down.shape[0]
    down = split_columns(down, n_xy)
    down = lax.all_to_all(down, XY, 0, 0, tiled=True).reshape(n_xy * cols, -1)

    gate, up, _ = lax.optimization_barrier((expert_gate[0], expert_up[0], spread))
    gate, up = stage(gate), stage(up)
    hid = hidden_units(experts, n_xy, mine, theirs, gain_sum, gate, up)
    units = hid.shape[3]
    hid = hid.reshape(2 * n_xy * group, units)
    hid_far = lax.ppermute(hid, "zh", FLIP)
    down = stage(down)
    hid_far, down = lax.optimization_barrier((hid_far, down))
    near = jnp.concatenate(
        [jnp.where(half == 0, hid, hid_far), jnp.where(half == 0, hid_far, hid)], axis=1
    )
    near = lax.all_gather(near, "core", axis=0, tiled=False)
    near = jnp.concatenate(
        [near[0, :, :units], near[1, :, :units], near[0, :, units:], near[1, :, units:]], axis=1
    )

    part = lax.dot_general(
        near, down, (((1,), (1,)), ((), ())), preferred_element_type=F32
    ).astype(BF16)
    part = part.reshape(n_xy, 2 * group, n_xy * cols)

    kv_cols = keyval_weights.shape[2] // experts

    def halve(acc, step):
        blocks = jnp.split(acc, acc.shape[1] // kv_cols, axis=1)
        even = jnp.concatenate(blocks[0::2], axis=1)
        odd = jnp.concatenate(blocks[1::2], axis=1)
        upper = (expert // step) % 2 == 1
        stay = jnp.where(upper, odd, even)
        leave = jnp.where(upper, even, odd)
        if len(blocks) == 2:
            leave = leave.astype(BF16)
        came = lax.ppermute(leave, "branch", [(b, b ^ step) for b in range(experts)])
        return stay, came

    def join(stay, came, after):
        came, _ = lax.optimization_barrier((came, after))
        return stay.astype(F32) + came.astype(F32)

    kv, _ = lax.optimization_barrier((keyval_weights[0], hid))
    kv = join(*halve(kv, steps[2]), part)
    kv = halve(kv, steps[1])

    part = lax.all_to_all(part, XY, 0, 0, tiled=True)
    total = jnp.sum(part.astype(F32), axis=0).astype(BF16)
    kv = join(*kv, total)
    total = lax.all_gather(total, "core", axis=0, tiled=False)
    spread = fan_out(experts, cap, total)
    kv, _ = lax.optimization_barrier((kv, spread))
    kv = join(*halve(kv, steps[0]), spread)
    slots = lax.all_to_all(spread, ZLINE, 0, 0, tiled=True)
    slots = slots.reshape(experts, 2, group, n_xy * cols)
    late_tokens, _ = lax.optimization_barrier((tokens, spread))
    merged_keyval = (kv / experts).astype(BF16)
    table, widened = mix_table(experts, cap, late_tokens, route_pair, weight_pair)
    mixed = mix_tokens(cols, table, widened, slots)
    return mixed, merged_keyval


def solution(mesh):
    n_x = n_y = int(round((mesh.devices.shape[1] // 4) ** 0.5))
    fine = Mesh(
        mesh.devices.reshape(mesh.devices.shape[0], n_x, n_y, 2, 2),
        ("branch", "x", "y", "zh", "core"),
    )
    in_specs = (
        P(DP, None),
        P(DP, None),
        P(DP, None),
        P("branch", None),
        P("branch", DP, None),
        P("branch", None, DP),
        P("branch", None, DP),
        P("branch", None, DP),
    )
    out_specs = (P(DP, None), P(DP, "branch"))
    return jax.shard_map(layer, mesh=fine, in_specs=in_specs, out_specs=out_specs, check_vma=False)
```
